32 devices in a mesh: wide: 16 (over z, y, core), narrow: 2 (over x).
Axes of the slice: x: 2, y: 2, z: 4, core: 2. Of those that a mesh axis runs over, the one named last changes fastest.
Arguments:
- hidden: bfloat16 [8192, 8192], P(('wide', 'narrow')), may hold values from -6 to 6
- key_grad: bfloat16 [8192, 512], P(('wide', 'narrow')), may hold values from -6 to 6
- positions: int32 [8192], P(('wide', 'narrow')), may hold values from 0 to 4095
- weight_codes: bfloat16 [8192, 512], P('narrow'), may hold values from -127 to 127
- weight_scales: bfloat16 [8192, 2], P('narrow'), may hold values from 9.9658966e-05 to 0.0009994507
- master: float32 [8192, 512], P(('narrow', 'wide')), may hold values from -0.0625 to 0.0625
- moment: float32 [8192, 512], P(('narrow', 'wide')), may hold values from -6 to 6
- second: float32 [8192, 512], P(('narrow', 'wide')), may hold values from 0.5 to 4
Outputs:
- keys_out: bfloat16 [8192, 512], P(('wide', 'narrow'))
- hidden_grad: bfloat16 [8192, 8192], P(('wide', 'narrow'))
- gradient: float32 [8192, 512], P(('narrow', 'wide'))
- master_out: float32 [8192, 512], P(('narrow', 'wide'))
- moment_out: float32 [8192, 512], P(('narrow', 'wide'))
- second_out: float32 [8192, 512], P(('narrow', 'wide'))
- new_codes: bfloat16 [8192, 512], P('narrow')
- new_scales: bfloat16 [8192, 2], P('narrow')
The draws below stay inside these ranges and needn't reach their ends.
All inputs are finite; a program needn't handle non-finite values.
Results may differ from the reference program's by a relative error of at most 0.025.
Values may be sent and summed in bfloat16 or wider, within the bound.
No kernel may reach another device: no remote copies, remote signals or barrier semaphores. Data moves between devices by JAX's collectives and lax.ppermute only.
A program may use at most 128 MiB of HBM per device.

```python
import math
import jax
import jax.numpy as jnp
from jax import lax

D = 8192
HEAD = 128
BLOCK = 256
TOK_DEV = 256
E = 512
BLOCKS = 2
TOKENS = 8192


def touch_ends(entries, rng, least, top_value):
    spot = [jax.random.randint(jax.random.fold_in(rng, axis), (), 0, length) for axis, length in enumerate(entries.shape)]
    longest = entries.shape.index(max(entries.shape))
    beside = spot[:longest] + [(spot[longest] + 1) % entries.shape[longest]] + spot[longest + 1:]
    return entries.at[tuple(spot)].set(least).at[tuple(beside)].set(top_value)


def with_spikes(result, rng, source, target, blocks, factor):
    owner, partner = [(jnp.arange(result.shape[dim]) // (result.shape[dim] // blocks)).reshape([-1 if axis == dim else 1 for axis in range(result.ndim)]) for dim in (source, target)]
    chosen = jax.random.permutation(rng, blocks)[partner]
    strong = (owner == chosen) | (owner == (partner + blocks // 2) % blocks)
    return jnp.where(strong, factor * result, result)


def block_scale(key, dims, pieces, low, high):
    level = 1.0
    for dim, parts in pieces:
        heights = jax.random.uniform(jax.random.fold_in(jax.random.fold_in(key, 6), dim), (parts,), jnp.float32, low / len(pieces), high / len(pieces))
        level = level * jnp.repeat(jnp.exp(heights), dims[dim] // parts).reshape((-1,) + (1,) * (len(dims) - 1 - dim))
    return level


def gaussian(stream_key, dims, scale, bound, split=(), held_as=jnp.bfloat16):
    entries = scale * jax.random.normal(stream_key, dims, jnp.float32)
    if split:
        entries = entries * block_scale(stream_key, dims, split, -0.22, 0.18)
    return jnp.clip(entries, -bound, bound).astype(held_as)


def heavy_noise(key, dims, deviation, reach, split, heavy, kind=jnp.bfloat16):
    drawn = deviation * jax.random.normal(key, dims, jnp.float32)
    if split:
        drawn = drawn * block_scale(key, dims, split, -0.22, 0.18)
    return jnp.clip(with_spikes(drawn, jax.random.fold_in(key, 3), *heavy), -reach, reach).astype(kind)


def setup_inputs(seed: int = 0) -> dict:
    streams_of = jax.random.split(jax.random.key(seed), 9)
    return {
        "hidden": heavy_noise(streams_of[0], (TOKENS, D), 1.0, 6.0, ((0, 32),), (0, 1, 32, 2.75)),
        "key_grad": gaussian(streams_of[1], (TOKENS, E), 1.0, 6.0, ((0, 32),)),
        "positions": touch_ends(jax.random.randint(streams_of[2], (TOKENS,), 0, 4096), jax.random.fold_in(streams_of[2], 1), 0, 4095).astype(jnp.int32),
        "weight_codes": jnp.clip(jax.random.uniform(streams_of[3], (D, E), jnp.float32, -127.0, 127.0) * block_scale(streams_of[3], (D, E), ((0, 2),), -0.4, 0.0), -127.0, 127.0).astype(jnp.bfloat16),
        "weight_scales": jnp.clip(jnp.exp(math.log(0.0009994507) - 2.3054518 * jax.random.uniform(streams_of[4], (D, BLOCKS), jnp.float32) ** block_scale(streams_of[4], (D, BLOCKS), ((0, 2),), -0.2, 0.2)), 9.965896606445312e-05, 0.0009994507).astype(jnp.bfloat16),
        "master": gaussian(streams_of[5], (D, E), D ** -0.5, 0.0625, ((0, 32),), jnp.float32),
        "moment": gaussian(streams_of[6], (D, E), 1.0, 6.0, ((0, 32),), jnp.float32),
        "second": jnp.clip(jnp.exp(math.log(4.0) - 2.0794415 * jax.random.uniform(streams_of[7], (D, E), jnp.float32) ** block_scale(streams_of[7], (D, E), ((0, 32),), -0.2, 0.2)), 0.5, 4.0),
    }


ROPE_BASE = 1000000.0
LEARN_RATE = 0.002
FIRST_DECAY = 0.9
SECOND_DECAY = 0.95
FIRST_FIX = 0.9999734386011124
SECOND_FIX = 0.994079470779666
ADAM_EPSILON = 1e-08
SCALE_EPSILON = 1e-06
CODE_RANGE = 127.0

def dequantize(weight_codes, weight_scales):
    height, width = weight_codes.shape
    blocks = weight_scales.shape[1]
    grouped = weight_codes.astype(jnp.float32).reshape(height, blocks, width // blocks)
    grouped = grouped * weight_scales.astype(jnp.float32)[:, :, None]
    return grouped.reshape(height, width).astype(jnp.bfloat16)

def rotation(positions, head_size):
    half_size = head_size // 2
    powers = jnp.arange(half_size, dtype=jnp.float32) * (-2.0 / head_size)
    frequency = jnp.power(jnp.float32(ROPE_BASE), powers)
    angles = positions.astype(jnp.float32)[:, None] * frequency[None, :]
    cosine = jnp.cos(angles)
    sines = jnp.sin(angles)
    return (jnp.concatenate([cosine, cosine], 1), jnp.concatenate([sines, sines], 1))

def turn_half(values):
    half_size = values.shape[-1] // 2
    return jnp.concatenate([-values[..., half_size:], values[..., :half_size]], -1)

def apply_rotation(values, cosine, sines, head_size):
    count, width = values.shape
    heads = values.reshape(count, width // head_size, head_size)
    turned = heads * cosine[:, None, :] + turn_half(heads) * sines[:, None, :]
    return turned.reshape(count, width)

def undo_rotation(values, cosine, sines, head_size):
    count, width = values.shape
    heads = values.reshape(count, width // head_size, head_size)
    scaled = heads * sines[:, None, :]
    reverted = heads * cosine[:, None, :] - turn_half(scaled)
    return reverted.reshape(count, width)

def adam_update(gradient, master, moment, second):
    moment_out = FIRST_DECAY * moment + (1.0 - FIRST_DECAY) * gradient
    second_out = SECOND_DECAY * second + (1.0 - SECOND_DECAY) * gradient * gradient
    step_size = moment_out / FIRST_FIX / (jnp.sqrt(second_out / SECOND_FIX) + ADAM_EPSILON)
    master_out = master - LEARN_RATE * step_size
    return (master_out, moment_out, second_out)

def requantize(master_out, block_width):
    height, width = master_out.shape
    grouped = master_out.reshape(height, width // block_width, block_width)
    peak = lax.optimization_barrier(jnp.max(jnp.abs(grouped), axis=2))
    new_scales = ((peak + SCALE_EPSILON) / CODE_RANGE).astype(jnp.bfloat16)
    divisor = lax.optimization_barrier(new_scales).astype(jnp.float32)
    new_codes = (grouped / divisor[:, :, None]).reshape(height, width).astype(jnp.bfloat16)
    return (new_codes, new_scales)

def reference(hidden, key_grad, positions, weight_codes, weight_scales, master, moment, second):
    weight = dequantize(weight_codes, weight_scales)
    cosine, sines = rotation(positions, HEAD)
    raw_keys = jnp.dot(hidden, weight, preferred_element_type=jnp.float32)
    keys_out = apply_rotation(raw_keys, cosine, sines, HEAD).astype(jnp.bfloat16)
    back_grad = undo_rotation(key_grad.astype(jnp.float32), cosine, sines, HEAD).astype(jnp.bfloat16)
    hidden_grad = lax.dot_general(back_grad, weight, (((1,), (1,)), ((), ())), preferred_element_type=jnp.float32).astype(jnp.bfloat16)
    block_count = TOKENS // TOK_DEV

    def add_block(running, inputs_pair):
        block_rows, block_back = inputs_pair
        partial_value = lax.dot_general(block_rows, block_back, (((0,), (0,)), ((), ())), preferred_element_type=jnp.float32).astype(jnp.bfloat16)
        partial_value = lax.optimization_barrier(partial_value)
        return (running + partial_value.astype(jnp.float32), None)
    summed, _ = lax.scan(add_block, jnp.zeros((D, E), jnp.float32), (hidden.reshape(block_count, TOK_DEV, D), back_grad.reshape(block_count, TOK_DEV, E)))
    gradient = summed / jnp.float32(block_count)
    master_out, moment_out, second_out = adam_update(gradient, master, moment, second)
    new_codes, new_scales = requantize(master_out, BLOCK)
    return (keys_out, hidden_grad, gradient, master_out, moment_out, second_out, new_codes, new_scales)
```

```python
import jax
import jax.numpy as jnp
from jax import lax
from jax.experimental import pallas as pl
from jax.experimental.pallas import tpu as pltpu
from jax.sharding import PartitionSpec as P

HEAD = 128
BLOCK = 256


ROPE_BASE = 1000000.0
LEARN_RATE = 0.002
FIRST_DECAY = 0.9
SECOND_DECAY = 0.95
FIRST_FIX = 0.9999734386011124
SECOND_FIX = 0.994079470779666
ADAM_EPSILON = 1e-08
SCALE_EPSILON = 1e-06
CODE_RANGE = 127.0


def dequantize(weight_codes, weight_scales):
    height, width = weight_codes.shape
    blocks = weight_scales.shape[1]
    grouped = weight_codes.astype(jnp.float32).reshape(height, blocks, width // blocks)
    grouped = grouped * weight_scales.astype(jnp.float32)[:, :, None]
    return grouped.reshape(height, width).astype(jnp.bfloat16)


def rotation(positions, head_size):
    half_size = head_size // 2
    powers = jnp.arange(half_size, dtype=jnp.float32) * (-2.0 / head_size)
    frequency = jnp.power(jnp.float32(ROPE_BASE), powers)
    angles = positions.astype(jnp.float32)[:, None] * frequency[None, :]
    cosine = jnp.cos(angles)
    sines = jnp.sin(angles)
    return (jnp.concatenate([cosine, cosine], 1), jnp.concatenate([sines, sines], 1))


def turn_half(values):
    half_size = values.shape[-1] // 2
    return jnp.concatenate([-values[..., half_size:], values[..., :half_size]], -1)


def apply_rotation(values, cosine, sines, head_size):
    count, width = values.shape
    heads = values.reshape(count, width // head_size, head_size)
    turned = heads * cosine[:, None, :] + turn_half(heads) * sines[:, None, :]
    return turned.reshape(count, width)


def undo_rotation(values, cosine, sines, head_size):
    count, width = values.shape
    heads = values.reshape(count, width // head_size, head_size)
    scaled = heads * sines[:, None, :]
    reverted = heads * cosine[:, None, :] - turn_half(scaled)
    return reverted.reshape(count, width)


def adam_update(gradient, master, moment, second):
    moment_out = FIRST_DECAY * moment + (1.0 - FIRST_DECAY) * gradient
    second_out = SECOND_DECAY * second + (1.0 - SECOND_DECAY) * gradient * gradient
    step_size = moment_out / FIRST_FIX / (jnp.sqrt(second_out / SECOND_FIX) + ADAM_EPSILON)
    master_out = master - LEARN_RATE * step_size
    return (master_out, moment_out, second_out)


def requantize(master_out, block_width):
    height, width = master_out.shape
    grouped = master_out.reshape(height, width // block_width, block_width)
    peak = jnp.max(jnp.abs(grouped), axis=2)
    new_scales = ((peak + SCALE_EPSILON) / CODE_RANGE).astype(jnp.bfloat16)
    divisor = lax.optimization_barrier(new_scales).astype(jnp.float32)
    new_codes = (grouped / divisor[:, :, None]).reshape(height, width).astype(jnp.bfloat16)
    return (new_codes, new_scales)


def shards(hidden, key_grad, positions, weight_codes, weight_scales, master, moment, second):
    narrow_count = lax.axis_size("narrow")
    wide_count = lax.axis_size("wide")
    devices_all = narrow_count * wide_count
    token_count = hidden.shape[0]
    cosine, sines = rotation(positions, HEAD)
    back_grad = undo_rotation(key_grad.astype(jnp.float32), cosine, sines, HEAD).astype(
        jnp.bfloat16
    )
    local_weight = dequantize(weight_codes, weight_scales)
    column_rows = lax.all_to_all(hidden, "narrow", split_axis=1, concat_axis=0, tiled=True)
    key_terms = jnp.dot(column_rows, local_weight, preferred_element_type=jnp.float32)
    raw_keys = lax.psum_scatter(
        key_terms.astype(jnp.bfloat16), "narrow", scatter_dimension=0, tiled=True
    ).astype(jnp.float32)
    keys_out = apply_rotation(raw_keys, cosine, sines, HEAD).astype(jnp.bfloat16)
    back_all = lax.all_gather(back_grad, "narrow", axis=0, tiled=True)
    column_grad = lax.dot_general(
        back_all, local_weight, (((1,), (1,)), ((), ())), preferred_element_type=jnp.float32
    ).astype(jnp.bfloat16)
    hidden_grad = lax.all_to_all(column_grad, "narrow", split_axis=0, concat_axis=1, tiled=True)
    part_width = column_rows.shape[1]
    partials = lax.dot_general(
        column_rows.reshape(narrow_count, token_count, part_width),
        back_all.reshape(narrow_count, token_count, back_all.shape[1]),
        (((1,), (1,)), ((0,), (0,))),
        preferred_element_type=jnp.float32,
    ).astype(jnp.bfloat16)
    partials = lax.optimization_barrier(partials)
    group_sum = jnp.sum(partials.astype(jnp.float32), axis=0)
    summed = lax.psum_scatter(
        group_sum.astype(jnp.bfloat16), "wide", scatter_dimension=0, tiled=True
    ).astype(jnp.float32)
    gradient = summed / jnp.float32(devices_all)
    master_out, moment_out, second_out = adam_update(gradient, master, moment, second)
    local_codes, local_scales = requantize(master_out, BLOCK)
    new_codes, new_scales = (
        lax.all_gather(local_codes, "wide", axis=0, tiled=True),
        lax.all_gather(local_scales, "wide", axis=0, tiled=True),
    )
    return (
        keys_out,
        hidden_grad,
        gradient,
        master_out,
        moment_out,
        second_out,
        new_codes,
        new_scales,
    )


AXES = ("wide", "narrow")
LANES = 128
CONTRACT_ROWS = (((0,), (0,)), ((), ()))
CONTRACT_COLS = (((1,), (1,)), ((), ()))


def full_spec(shape):
    return pl.BlockSpec(shape, lambda *_: (0,) * len(shape))


def cost(flops, moved):
    return pl.CostEstimate(flops=int(flops), bytes_accessed=int(moved), transcendentals=0)


def call(kernel, meta, grid, in_specs, out_specs, out_shape, operands, name, flops, moved,
         scratch=(), aliases=None):
    return pl.pallas_call(
        kernel,
        grid_spec=pltpu.PrefetchScalarGridSpec(
            num_scalar_prefetch=1, grid=grid, in_specs=in_specs, out_specs=out_specs,
            scratch_shapes=list(scratch),
        ),
        out_shape=out_shape,
        input_output_aliases=aliases or {},
        cost_estimate=cost(flops, moved),
        name=name,
    )(meta, *operands)


X, CORE, Y, Z0, Z1 = range(5)


def pick_kernel(meta, hidden_ref, out_ref):
    rows = out_ref.shape[1] // 4
    other = 1 - meta[CORE]
    for k in range(4):
        start = pl.multiple_of(k * 2 * rows + other * rows, rows)
        out_ref[:, k * rows:(k + 1) * rows] = hidden_ref[:, pl.ds(start, rows)]


def pick_columns(meta, hidden, rows):
    tokens, width = hidden.shape
    step = 8 * rows
    return call(
        pick_kernel, meta, (width // step,),
        [pl.BlockSpec((tokens, step), lambda i, m: (0, i))],
        pl.BlockSpec((tokens, step // 2), lambda i, m: (0, i)),
        jax.ShapeDtypeStruct((tokens, width // 2), hidden.dtype),
        (hidden,), "pick_columns", 0, hidden.size * 3,
    )


def back_kernel(meta, grad_ref, cos_ref, sin_ref, out_ref):
    for h in range(grad_ref.shape[1] // HEAD):
        part = grad_ref[:, h * HEAD:(h + 1) * HEAD].astype(jnp.float32)
        turned = pltpu.roll(part, HEAD // 2, 1)
        out_ref[:, h * HEAD:(h + 1) * HEAD] = (
            part * cos_ref[...] + turned * sin_ref[...]
        ).astype(out_ref.dtype)


def back_rotate(meta, key_grad, cosine, signed):
    return call(
        back_kernel, meta, (1,),
        [full_spec(key_grad.shape), full_spec(cosine.shape), full_spec(signed.shape)],
        full_spec(key_grad.shape),
        jax.ShapeDtypeStruct(key_grad.shape, jnp.bfloat16),
        (key_grad, cosine, signed), "back_rotate", 0, key_grad.size * 8,
    )


def partial_kernel(side, meta, own_ref, peer_ref, bown_ref, bpeer_ref, first_ref, second_ref):
    i = pl.program_id(0)
    rows = first_ref.shape[-2]
    half = first_ref.shape[-1]
    core = meta[CORE]

    def product(ry, rz0, column):
        k = ((meta[Z0] ^ rz0) << 1) | (meta[Y] ^ ry)
        own = own_ref[:, pl.ds(pl.multiple_of(k * 2 * rows + core * rows, rows), rows)]
        peer = peer_ref[:, pl.ds(pl.multiple_of(k * rows, rows), rows)]
        total = lax.dot_general(
            own, bown_ref[:, column:column + half], CONTRACT_ROWS,
            preferred_element_type=jnp.float32,
        ) + lax.dot_general(
            peer, bpeer_ref[:, column:column + half], CONTRACT_ROWS,
            preferred_element_type=jnp.float32,
        )
        return total.astype(jnp.bfloat16)

    @pl.when(i < 2)
    def _():
        for ry in range(2):
            for rz0 in range(2):
                first_ref[ry, rz0, 0] = product(ry, rz0, 0)

    for rz0 in range(2):
        second_ref[0, rz0, 0] = product(side, rz0, half)


def partial_blocks(side, meta, hidden, peer_hidden, back, peer_back, rows):
    tokens, width = hidden.shape
    features = back.shape[1]
    half = features // 2
    step = 8 * rows

    def place(i, m):
        rx = side ^ (i >> 1)
        rz1 = 1 ^ (i & 1)
        return ((m[X] ^ rx) << 1) | (m[Z1] ^ rz1)

    shape = (2, 2, 2, rows, half)
    out = jax.ShapeDtypeStruct(shape, jnp.bfloat16)
    flops = width * features * tokens
    return call(
        lambda *refs: partial_kernel(side, *refs), meta, (4,),
        [
            pl.BlockSpec((tokens, step), lambda i, m: (0, place(i, m))),
            pl.BlockSpec((tokens, step // 2), lambda i, m: (0, place(i, m))),
            full_spec(back.shape), full_spec(back.shape),
        ],
        [
            pl.BlockSpec((2, 2, 1, rows, half), lambda i, m: (0, 0, 1 - jnp.minimum(i, 1), 0, 0)),
            pl.BlockSpec((1, 2, 1, rows, half), lambda i, m: (side ^ (i >> 1), 0, 1 ^ (i & 1), 0, 0)),
        ],
        [out, out],
        (hidden, peer_hidden, back, peer_back), "partial_blocks", flops, hidden.size * 5,
    )


def project_step(codes, hidden_ref, scales_ref, back_ref, total_ref, grad_ref):
    block = codes.shape[1] // scales_ref.shape[0]
    result = None
    for b in range(scales_ref.shape[0]):
        part = codes[:, b * block:(b + 1) * block]
        scale = scales_ref[b:b + 1, :]
        scaled = hidden_ref[...] * scale
        total_ref[:, b * block:(b + 1) * block] += jnp.dot(
            scaled, part, preferred_element_type=jnp.float32
        )
        term = lax.dot_general(
            back_ref[:, b * block:(b + 1) * block], part, CONTRACT_COLS,
            preferred_element_type=jnp.float32,
        ) * scale.astype(jnp.float32)
        result = term if result is None else result + term
    grad_ref[...] = result.astype(grad_ref.dtype)


def own_kernel(meta, codes_ref, hidden_ref, scales_ref, back_ref, total_ref, grad_ref):
    @pl.when(pl.program_id(0) == 0)
    def _():
        total_ref[...] = jnp.zeros_like(total_ref)

    project_step(codes_ref[...], hidden_ref, scales_ref, back_ref, total_ref, grad_ref)


def project_own(meta, codes, scales_t, hidden, back):
    height, features = codes.shape
    tokens = hidden.shape[0]
    step = height // 4
    return call(
        own_kernel, meta, (4,),
        [
            pl.BlockSpec((step, features), lambda i, m: (i, 0)),
            pl.BlockSpec((tokens, step), lambda i, m: (0, m[X] * 4 + i)),
            pl.BlockSpec((scales_t.shape[0], step), lambda i, m: (0, i)),
            full_spec(back.shape),
        ],
        [
            full_spec((tokens, features)),
            pl.BlockSpec((tokens, step), lambda i, m: (0, m[X] * 4 + i)),
        ],
        [
            jax.ShapeDtypeStruct((tokens, features), jnp.float32),
            jax.ShapeDtypeStruct(hidden.shape, jnp.bfloat16),
        ],
        (codes, hidden, scales_t, back), "project_own",
        4 * tokens * height * features, codes.size * 2 + hidden.size * 2,
    )


def other_kernel(owners, last, meta, *refs):
    count = len(set(owners))
    sources = refs[:count]
    hidden_ref, scales_ref, back_ref, cos_ref, sin_ref, sum_ref, _, total_ref, grad_ref, work_ref = refs[count:]
    i = pl.program_id(0)

    @pl.when(i == 0)
    def _():
        work_ref[...] = sum_ref[...]

    for s in range(count):
        steps = [n for n, owner in enumerate(owners) if owner == s]

        @pl.when((i >= steps[0]) & (i <= steps[-1]))
        def _():
            project_step(sources[s][...], hidden_ref, scales_ref, back_ref, work_ref, grad_ref)

    @pl.when(i == len(owners) - 1)
    def _():
        if last:
            for h in range(total_ref.shape[1] // HEAD):
                part = work_ref[:, h * HEAD:(h + 1) * HEAD]
                turned = pltpu.roll(part, HEAD // 2, 1)
                total_ref[:, h * HEAD:(h + 1) * HEAD] = (
                    part * cos_ref[...] - turned * sin_ref[...]
                ).astype(total_ref.dtype)
        else:
            total_ref[...] = work_ref[...]


def project_other(meta, sources, units, scales_t, hidden, back, cosine, signed, total, grad, last):
    features = back.shape[1]
    tokens = hidden.shape[0]
    unit = scales_t.shape[1] // 8
    owners = []
    for s, source in enumerate(sources):
        owners += [s] * (source.shape[0] // unit)

    def source_spec(s):
        first = owners.index(s)
        top = owners.count(s) - 1
        return pl.BlockSpec((unit, features), lambda i, m: (jnp.clip(i - first, 0, top), 0))

    place = lambda i, m: (0, (1 - m[X]) * 8 + units(i, m))
    count = len(sources)
    kind = jnp.bfloat16 if last else jnp.float32
    return call(
        lambda *refs: other_kernel(owners, last, *refs), meta, (len(owners),),
        [source_spec(s) for s in range(count)] + [
            pl.BlockSpec((tokens, unit), place),
            pl.BlockSpec((scales_t.shape[0], unit), lambda i, m: (0, units(i, m))),
            full_spec(back.shape), full_spec(cosine.shape), full_spec(signed.shape),
            full_spec(total.shape),
            pl.BlockSpec(memory_space=pl.ANY),
        ],
        [full_spec(total.shape), pl.BlockSpec((tokens, unit), place)],
        [
            jax.ShapeDtypeStruct(total.shape, kind),
            jax.ShapeDtypeStruct(grad.shape, grad.dtype),
        ],
        (*sources, hidden, scales_t, back, cosine, signed, total, grad), "project_other",
        4 * tokens * unit * len(owners) * features, len(owners) * unit * (features + 2 * tokens) * 2,
        scratch=[pltpu.VMEM(total.shape, jnp.float32)],
        aliases={1 + count + 6: 1},
    )


def adam_kernel(devices, meta, first_ref, first_in, second_ref, second_in, master_ref, moment_ref,
                square_ref, gradient_out, master_out, moment_out, square_out, message_out):
    rows = master_ref.shape[0]
    half = master_ref.shape[1] // 2
    for b, (kept, came) in enumerate(((first_ref, first_in), (second_ref, second_in))):
        columns = slice(b * half, (b + 1) * half)
        summed = kept[...].astype(jnp.float32) + came[...].astype(jnp.float32)
        gradient = summed / jnp.float32(devices)
        updated, moment, square = adam_update(
            gradient, master_ref[:, columns], moment_ref[:, columns], square_ref[:, columns]
        )
        gradient_out[:, columns] = gradient
        master_out[:, columns] = updated
        moment_out[:, columns] = moment
        square_out[:, columns] = square
        peak = jnp.max(jnp.abs(updated), axis=1, keepdims=True)
        scale = ((peak + SCALE_EPSILON) / CODE_RANGE).astype(jnp.bfloat16).astype(jnp.float32)
        message_out[:rows, columns] = (updated / scale).astype(jnp.bfloat16)
        across = jnp.transpose(jnp.broadcast_to(scale, (rows, LANES)))
        message_out[rows:, columns] = across[:message_out.shape[0] - rows].astype(jnp.bfloat16)


def adam_step(meta, devices, first, first_in, second, second_in, master, moment, square):
    rows, features = master.shape
    plain = jax.ShapeDtypeStruct(master.shape, jnp.float32)
    message = (rows + 16, features)
    return call(
        lambda *refs: adam_kernel(devices, *refs), meta, (1,),
        [full_spec(first.shape)] * 4 + [full_spec(master.shape)] * 3,
        [full_spec(master.shape)] * 4 + [full_spec(message)],
        [plain] * 4 + [jax.ShapeDtypeStruct(message, jnp.bfloat16)],
        (first, first_in, second, second_in, master, moment, square), "adam_step",
        0, master.size * 40,
    )


def assemble_kernel(rows, meta, *refs):
    messages = refs[:16]
    codes_out, scales_out, codes_buf, lines_buf, scales_buf, in_sem, out_sem = refs[16:]
    place = []
    for n in range(16):
        rc, ry, rz0, rz1 = n >> 3, (n >> 2) & 1, (n >> 1) & 1, n & 1
        place.append(
            ((meta[Z1] ^ rz1) << 3) | ((meta[Z0] ^ rz0) << 2) | ((meta[Y] ^ ry) << 1)
            | (meta[CORE] ^ rc)
        )

    def span(n):
        return pl.ds(pl.multiple_of(place[n] * rows, rows), rows)

    def load(n):
        return (
            pltpu.make_async_copy(messages[n].at[pl.ds(0, rows)], codes_buf.at[span(n)], in_sem.at[n, 0]),
            pltpu.make_async_copy(messages[n].at[pl.ds(rows, 16)], lines_buf.at[n], in_sem.at[n, 1]),
        )

    def store(n):
        return pltpu.make_async_copy(codes_buf.at[span(n)], codes_out.at[span(n)], out_sem.at[n])

    for n in range(16):
        for copy in load(n):
            copy.start()
    for n in range(16):
        for copy in load(n):
            copy.wait()
        store(n).start()
        half = lines_buf.shape[2] // 2
        for b in range(2):
            scales_buf[b:b + 1, span(n)] = lines_buf[n, 0:16, b * half:(b + 1) * half].astype(
                jnp.float32
            )[0:1]
    scales_out[...] = scales_buf[...].astype(scales_out.dtype)
    for n in range(16):
        store(n).wait()


def assemble(meta, messages, rows, features):
    height = 16 * rows
    return call(
        lambda *refs: assemble_kernel(rows, *refs), meta, (1,),
        [pl.BlockSpec(memory_space=pl.ANY)] * 16,
        [pl.BlockSpec(memory_space=pl.ANY), full_spec((2, height))],
        [
            jax.ShapeDtypeStruct((height, features), jnp.bfloat16),
            jax.ShapeDtypeStruct((2, height), jnp.bfloat16),
        ],
        tuple(messages), "assemble", 0, height * features * 8,
        scratch=[
            pltpu.VMEM((height, features), jnp.bfloat16),
            pltpu.VMEM((16, 16, features), jnp.bfloat16),
            pltpu.VMEM((2, height), jnp.float32),
            pltpu.SemaphoreType.DMA((16, 2)),
            pltpu.SemaphoreType.DMA((16,)),
        ],
    )


def tables(positions):
    lane = jnp.arange(HEAD, dtype=jnp.int32)
    half = HEAD // 2
    powers = (lane % half).astype(jnp.float32) * (-2.0 / HEAD)
    frequency = jnp.power(jnp.float32(ROPE_BASE), powers)
    angles = positions.astype(jnp.float32)[:, None] * frequency[None, :]
    sines = jnp.sin(angles)
    return jnp.cos(angles), jnp.where(lane < half, sines, -sines)


def after(value, *others):
    return lax.optimization_barrier((value, *others))[0]


def pairwise(hidden, key_grad, positions, weight_codes, weight_scales, master, moment, second):
    narrow_count = lax.axis_size("narrow")
    wide_count = lax.axis_size("wide")
    devices = narrow_count * wide_count
    rows, features = master.shape

    def swap(value, wide_mask, narrow_mask=0):
        pairs = []
        for w in range(wide_count):
            for n in range(narrow_count):
                pairs.append((w * narrow_count + n, (w ^ wide_mask) * narrow_count + (n ^ narrow_mask)))
        return lax.ppermute(value, AXES, pairs)

    over_core = lambda v: swap(v, 1)
    over_y = lambda v: swap(v, 2)
    over_z0 = lambda v: swap(v, 4)
    over_z1 = lambda v: swap(v, 8)
    over_x = lambda v: swap(v, 0, 1)

    wide, narrow = lax.axis_index("wide"), lax.axis_index("narrow")
    slot = jnp.arange(8, dtype=jnp.int32)
    meta = jnp.where(slot == 0, narrow, (wide >> jnp.maximum(slot - 1, 0)) & 1).astype(jnp.int32)
    core, z0 = wide & 1, (wide >> 2) & 1
    scales_t = weight_scales.T
    height = weight_codes.shape[0]
    unit = height // 8

    early = lax.dynamic_slice_in_dim(weight_codes, (core * 4 + z0) * unit, unit, 0)
    early_x = over_x(early)
    other_scales = over_x(scales_t)

    picked = pick_columns(meta, hidden, rows)
    peer_hidden = over_core(picked)
    cosine, signed = tables(positions)
    back = back_rotate(meta, key_grad, cosine, signed)
    peer_back = over_core(back)

    first_send, second_send = partial_blocks(1, meta, hidden, peer_hidden, back, peer_back, rows)
    first_came = over_x(first_send)
    second_came = over_y(second_send)
    early_z = over_z0(early_x)
    first_keep, second_keep = partial_blocks(0, meta, hidden, peer_hidden, back, peer_back, rows)
    early_x_peer = over_core(early_x)
    total, grad = project_own(meta, weight_codes, scales_t, hidden, back)
    early_z_peer = over_core(early_z)

    first2 = over_y(first_keep[1] + first_came[1])
    second2 = over_x(second_keep[1] + second_came[1])
    first3 = first_keep[0] + first_came[0]
    second3 = second_keep[0] + second_came[0]

    def early_unit(i, m):
        return ((m[CORE] ^ (i >> 1)) << 2) | (m[Z0] ^ (i & 1))

    total, grad = project_other(
        meta, (early_x, early_z, early_x_peer, early_z_peer), early_unit, other_scales, hidden, back,
        cosine, signed, total, grad, False,
    )

    late = lax.dynamic_slice_in_dim(
        after(weight_codes, second2), (core * 4 + 2) * unit, 2 * unit, 0
    )
    late_x = over_x(late)

    first4 = over_z0(first3[1] + first2[1])
    second4 = over_z0(second3[1] + second2[1])
    first5 = first3[0] + first2[0]
    second5 = second3[0] + second2[0]
    first6 = over_z1(first5[1] + first4[1])
    second6 = over_z1(second5[1] + second4[1])
    first7 = first5[0] + first4[0]
    second7 = second5[0] + second4[0]

    gradient, master_out, moment_out, second_out, message = adam_step(
        meta, devices, first7, first6, second7, second6, master, moment, second
    )
    from_z1 = over_z1(message)
    plane = [message, from_z1]
    plane += [over_z0(v) for v in plane]
    plane += [over_y(v) for v in plane]
    plane += [over_core(v) for v in plane]
    new_codes, new_scales = assemble(meta, plane, rows, features)

    late_peer = over_core(late_x)

    def late_unit(i, m):
        return ((m[CORE] ^ (i >> 1)) << 2) | 2 | (i & 1)

    keys_out, hidden_grad = project_other(
        meta, (late_x, late_peer), late_unit, other_scales, hidden, back, cosine, signed, total, grad,
        True,
    )
    return (
        keys_out, hidden_grad, gradient, master_out, moment_out, second_out, new_codes, new_scales.T,
    )


def by_pairs(mesh, rows, features):
    return (
        mesh.shape["narrow"] == 2 and mesh.shape["wide"] == 16
        and rows % 256 == 0 and features == 2 * BLOCK
    )


def solution(mesh):
    in_specs = (
        P(("wide", "narrow"), None),
        P(("wide", "narrow"), None),
        P(("wide", "narrow")),
        P("narrow", None),
        P("narrow", None),
        P(("narrow", "wide"), None),
        P(("narrow", "wide"), None),
        P(("narrow", "wide"), None),
    )
    out_specs = (
        P(("wide", "narrow"), None),
        P(("wide", "narrow"), None),
        P(("narrow", "wide"), None),
        P(("narrow", "wide"), None),
        P(("narrow", "wide"), None),
        P(("narrow", "wide"), None),
        P("narrow", None),
        P("narrow", None),
    )
    def run(*arrays):
        devices = mesh.shape["narrow"] * mesh.shape["wide"]
        height, features = arrays[3].shape
        body = pairwise if by_pairs(mesh, height // devices, features) else shards
        return jax.shard_map(
            body, mesh=mesh, in_specs=in_specs, out_specs=out_specs, check_vma=False
        )(*arrays)

    return run
```
